32 devices in a mesh: seq: 2 (over x), fsdp: 2 (over y), ctx: 8 (over z, core).
Axes of the slice: x: 2, y: 2, z: 4, core: 2. Of those that a mesh axis runs over, the one named last changes fastest.
Arguments:
- tokens: bfloat16 [4, 1024, 960], P(('seq', 'fsdp'), 'ctx'), may hold values from -6 to 6
- cotangent: bfloat16 [4, 1024, 960], P(('seq', 'fsdp'), 'ctx'), may hold values from -6 to 6
- block_order: int32 [16], replicated, may hold values from 0 to 15, each once
- gain_attn: float32 [960], replicated, may hold values from 0.5 to 1.5
- gain_mlp: float32 [960], replicated, may hold values from 0.5 to 1.5
- w_query: bfloat16 [960, 960], P(('seq', 'fsdp'), 'ctx'), may hold values from -0.1875 to 0.1875
- w_key: bfloat16 [960, 320], P(('seq', 'fsdp'), 'ctx'), may hold values from -0.1875 to 0.1875
- w_value: bfloat16 [960, 320], P(('seq', 'fsdp'), 'ctx'), may hold values from -0.1875 to 0.1875
- w_out: bfloat16 [960, 960], P(('seq', 'fsdp'), 'ctx'), may hold values from -3 to 3
- w_gate: bfloat16 [960, 2560], P(('seq', 'fsdp'), 'ctx'), may hold values from -0.1875 to 0.1875
- w_up: bfloat16 [960, 2560], P(('seq', 'fsdp'), 'ctx'), may hold values from -0.1875 to 0.1875
- w_down: bfloat16 [2560, 960], P(('seq', 'fsdp'), 'ctx'), may hold values from -0.125 to 0.125
Outputs:
- output: bfloat16 [4, 1024, 960], P(('seq', 'fsdp'), 'ctx')
- input_grad: bfloat16 [4, 1024, 960], P(('seq', 'fsdp'), 'ctx')
- gain_attn_grad: float32 [960], replicated
- gain_mlp_grad: float32 [960], replicated
- query_grad: float32 [960, 960], P(('seq', 'fsdp'), 'ctx')
- key_grad: float32 [960, 320], P(('seq', 'fsdp'), 'ctx')
- value_grad: float32 [960, 320], P(('seq', 'fsdp'), 'ctx')
- out_grad: float32 [960, 960], P(('seq', 'fsdp'), 'ctx')
- gate_grad: float32 [960, 2560], P(('seq', 'fsdp'), 'ctx')
- up_grad: float32 [960, 2560], P(('seq', 'fsdp'), 'ctx')
- down_grad: float32 [2560, 960], P(('seq', 'fsdp'), 'ctx')
The draws below stay inside these ranges and needn't reach their ends.
Inputs may be any that keep to these rules, and one draw needn't show every extreme that they name: block_order names each block number of one sequence once.
All inputs are finite; a program needn't handle non-finite values.
Results may differ from the reference program's by a relative error of at most 0.023.
Values may be sent and summed in bfloat16 or wider, within the bound.
A program may use at most 128 MiB of HBM per device.

```python
import math
import jax
import jax.numpy as jnp
from jax import lax

D = 960
HEADS = 15
KV_HEADS = 5
HEAD_DIM = 64
FF = 2560
BLK = 64
BLOCKS = 16
SEQ_LEN = 1024
SEQS = 4


def block_scale(stream_key, extent, split, low, high):
    factor_of, own = 1.0, jax.random.fold_in(stream_key, 6)
    for axis_at, shards_of in split:
        draws = jnp.exp(jax.random.uniform(jax.random.fold_in(own, axis_at), (shards_of,), jnp.float32, low / len(split), high / len(split)))
        factor_of = factor_of * jnp.repeat(draws, extent[axis_at] // shards_of).reshape([-1 if axis == axis_at else 1 for axis in range(len(extent))])
    return factor_of


def noise(own_key, dims, deviation, reach, split=(), kind=jnp.bfloat16):
    array = deviation * jax.random.normal(own_key, dims, jnp.float32)
    if split:
        array = array * block_scale(own_key, dims, split, -0.22, 0.18)
    return jnp.clip(array, -reach, reach).astype(kind)


def setup_inputs(seed: int = 0) -> dict:
    splits = jax.random.split(jax.random.key(seed), 13)
    tokens = noise(splits[0], (SEQS, SEQ_LEN, D), 1.0, 6.0, ((0, 4), (1, 8)))
    cotangent = noise(splits[1], (SEQS, SEQ_LEN, D), 1.0, 6.0, ((0, 4), (1, 8)))
    block_order = jax.random.permutation(splits[2], BLOCKS).astype(jnp.int32)
    gain_attn = jnp.clip(1.0 + 0.1 * jax.random.normal(splits[3], (D,), jnp.float32), 0.5, 1.5)
    gain_mlp = jnp.clip(1.0 + 0.1 * jax.random.normal(splits[4], (D,), jnp.float32), 0.5, 1.5)
    w_query = noise(splits[5], (D, HEADS * HEAD_DIM), D ** -0.5, 0.1875, ((0, 4), (1, 8)))
    w_key = noise(splits[6], (D, KV_HEADS * HEAD_DIM), D ** -0.5, 0.1875, ((0, 4), (1, 8)))
    w_value = noise(splits[7], (D, KV_HEADS * HEAD_DIM), D ** -0.5, 0.1875, ((0, 4), (1, 8)))
    w_out = noise(splits[8], (HEADS * HEAD_DIM, D), 4 ** -0.5, 3.0, ((0, 4), (1, 8)))
    w_gate = noise(splits[9], (D, FF), D ** -0.5, 0.1875, ((0, 4), (1, 8)))
    w_up = noise(splits[10], (D, FF), D ** -0.5, 0.1875, ((0, 4), (1, 8)))
    w_down = noise(splits[11], (FF, D), FF ** -0.5, 0.125, ((0, 4), (1, 8)))
    return {"tokens": tokens, "cotangent": cotangent, "block_order": block_order, "gain_attn": gain_attn, "gain_mlp": gain_mlp, "w_query": w_query, "w_key": w_key, "w_value": w_value, "w_out": w_out, "w_gate": w_gate, "w_up": w_up, "w_down": w_down}


rope_base = 100000.0
norm_eps = 1e-05

def rope_tables(positions, half_dim):
    freq_index = jnp.arange(half_dim, dtype=jnp.float32)
    inverse = rope_base ** (-freq_index / half_dim)
    angles = positions.astype(jnp.float32)[:, None] * inverse[None, :]
    return (jnp.cos(angles), jnp.sin(angles))

def rotate(values, cosine, sine):
    half_dim = values.shape[-1] // 2
    first_half = values[..., :half_dim]
    second_half = values[..., half_dim:]
    cos_part = cosine[:, None, :]
    sin_part = sine[:, None, :]
    return jnp.concatenate([first_half * cos_part - second_half * sin_part, second_half * cos_part + first_half * sin_part], axis=-1)

def rotate_back(grads, cosine, sine):
    half_dim = grads.shape[-1] // 2
    first_half = grads[..., :half_dim]
    second_half = grads[..., half_dim:]
    cos_part = cosine[:, None, :]
    sin_part = sine[:, None, :]
    return jnp.concatenate([first_half * cos_part + second_half * sin_part, second_half * cos_part - first_half * sin_part], axis=-1)

def as_rounded(values):
    return lax.optimization_barrier(values.astype(jnp.bfloat16)).astype(jnp.float32)

def norm_forward(values, gain):
    inverse_rms = lax.rsqrt(lax.optimization_barrier(jnp.mean(values * values, axis=1, keepdims=True)) + norm_eps)
    scaled = values * inverse_rms
    return (inverse_rms, scaled, (scaled * gain).astype(jnp.bfloat16))

def norm_backward(grad_in, inverse_rms, scaled, gain):
    weighted = grad_in * gain
    back = inverse_rms * (weighted - scaled * lax.optimization_barrier(jnp.mean(weighted * scaled, axis=1, keepdims=True)))
    return (back, lax.optimization_barrier(jnp.sum(grad_in * scaled, axis=0)))

def attend(query_rot, key_rot, value_b, positions):
    seq_len = query_rot.shape[0]
    block_rows = min(512, seq_len)
    num_blocks = seq_len // block_rows
    group_size = HEADS // KV_HEADS
    scale = 1.0 / math.sqrt(HEAD_DIM)
    key_all = key_rot.astype(jnp.float32).reshape(seq_len, KV_HEADS, HEAD_DIM)
    value_all = value_b.astype(jnp.float32).reshape(seq_len, KV_HEADS, HEAD_DIM)

    def one_block(carry, inputs):
        query_block, pos_block = inputs
        query_group = query_block.astype(jnp.float32).reshape(block_rows, KV_HEADS, group_size, HEAD_DIM)
        scores = jnp.einsum('rgjd,kgd->gjrk', query_group, key_all) * scale
        causal_mask = positions[None, :] <= pos_block[:, None]
        exp_sum = lax.optimization_barrier(jnp.sum(jnp.where(causal_mask, jnp.exp(scores), 0.0), axis=-1))
        log_total = jnp.log(exp_sum)
        prob_bf = as_rounded(jnp.where(causal_mask, jnp.exp(scores - log_total[..., None]), 0.0))
        attn_out = jnp.einsum('gjrk,kgd->rgjd', prob_bf, value_all)
        return (carry, (log_total, attn_out.reshape(block_rows, HEADS * HEAD_DIM).astype(jnp.bfloat16)))
    unused, (log_total, attn_out) = lax.scan(one_block, jnp.zeros((), jnp.float32), (query_rot.reshape(num_blocks, block_rows, HEADS * HEAD_DIM), positions.reshape(num_blocks, block_rows)))
    return (log_total, attn_out.reshape(seq_len, HEADS * HEAD_DIM))

def attend_back(query_rot, key_rot, value_b, attn_out, grad_out, log_total, positions):
    seq_len = query_rot.shape[0]
    block_rows = min(512, seq_len)
    num_blocks = seq_len // block_rows
    group_size = HEADS // KV_HEADS
    scale = 1.0 / math.sqrt(HEAD_DIM)
    key_all = key_rot.astype(jnp.float32).reshape(seq_len, KV_HEADS, HEAD_DIM)
    value_all = value_b.astype(jnp.float32).reshape(seq_len, KV_HEADS, HEAD_DIM)

    def one_block(carry, inputs):
        key_grad, value_grad = carry
        query_block, out_block, grad_block, log_block, pos_block = inputs
        query_group = query_block.astype(jnp.float32).reshape(block_rows, KV_HEADS, group_size, HEAD_DIM)
        grad_group = grad_block.astype(jnp.float32).reshape(block_rows, KV_HEADS, group_size, HEAD_DIM)
        out_group = out_block.astype(jnp.float32).reshape(block_rows, KV_HEADS, group_size, HEAD_DIM)
        row_delta = jnp.transpose(lax.optimization_barrier(jnp.sum(grad_group * out_group, axis=-1)), (1, 2, 0))
        scores = jnp.einsum('rgjd,kgd->gjrk', query_group, key_all) * scale
        causal_mask = positions[None, :] <= pos_block[:, None]
        probs_full = jnp.where(causal_mask, jnp.exp(scores - log_block[..., None]), 0.0)
        prob_bf = as_rounded(probs_full)
        prod_grad = jnp.einsum('rgjd,kgd->gjrk', grad_group, value_all)
        score_grad = as_rounded(probs_full * (prod_grad - row_delta[..., None]) * scale)
        query_grad = jnp.einsum('gjrk,kgd->rgjd', score_grad, key_all)
        key_grad = key_grad + jnp.einsum('gjrk,rgjd->kgd', score_grad, query_group)
        value_grad = value_grad + jnp.einsum('gjrk,rgjd->kgd', prob_bf, grad_group)
        return ((key_grad, value_grad), query_grad.reshape(block_rows, HEADS, HEAD_DIM))
    start_grads = (jnp.zeros((seq_len, KV_HEADS, HEAD_DIM), jnp.float32), jnp.zeros((seq_len, KV_HEADS, HEAD_DIM), jnp.float32))
    shaped = (query_rot.reshape(num_blocks, block_rows, HEADS * HEAD_DIM), attn_out.reshape(num_blocks, block_rows, HEADS * HEAD_DIM), grad_out.reshape(num_blocks, block_rows, HEADS * HEAD_DIM), log_total, positions.reshape(num_blocks, block_rows))
    (key_grad, value_grad), query_grad = lax.scan(one_block, start_grads, shaped)
    return (query_grad.reshape(seq_len, HEADS, HEAD_DIM), key_grad, value_grad)

def reference(tokens, cotangent, block_order, gain_attn, gain_mlp, w_query, w_key, w_value, w_out, w_gate, w_up, w_down):
    slot_index = jnp.arange(SEQ_LEN, dtype=jnp.int32)
    positions = (block_order[slot_index // BLK] * BLK + slot_index % BLK).astype(jnp.int32)
    cosine, sine = rope_tables(positions, HEAD_DIM // 2)

    def one_sequence(carry, inputs):
        token_seq, cot_seq = inputs
        token_f32 = token_seq.astype(jnp.float32)
        rms_attn, unit_attn, normed_attn = norm_forward(token_f32, gain_attn)
        query_raw = jnp.dot(normed_attn, w_query, preferred_element_type=jnp.float32).reshape(SEQ_LEN, HEADS, HEAD_DIM)
        key_raw = jnp.dot(normed_attn, w_key, preferred_element_type=jnp.float32).reshape(SEQ_LEN, KV_HEADS, HEAD_DIM)
        value_raw = jnp.dot(normed_attn, w_value, preferred_element_type=jnp.float32)
        query_rot = rotate(query_raw, cosine, sine).reshape(SEQ_LEN, HEADS * HEAD_DIM).astype(jnp.bfloat16)
        key_rot = rotate(key_raw, cosine, sine).reshape(SEQ_LEN, KV_HEADS * HEAD_DIM).astype(jnp.bfloat16)
        value_b = value_raw.astype(jnp.bfloat16)
        log_total, attn_bf = attend(query_rot, key_rot, value_b, positions)
        middle = token_f32 + jnp.dot(attn_bf, w_out, preferred_element_type=jnp.float32)
        rms_mlp, unit_mlp, normed_mlp = norm_forward(middle, gain_mlp)
        gate_pre = jnp.dot(normed_mlp, w_gate, preferred_element_type=jnp.float32)
        up_pre = jnp.dot(normed_mlp, w_up, preferred_element_type=jnp.float32)
        sigmoid_gate = jax.nn.sigmoid(gate_pre)
        silu_gate = gate_pre * sigmoid_gate
        hidden = (silu_gate * up_pre).astype(jnp.bfloat16)
        result = (middle + jnp.dot(hidden, w_down, preferred_element_type=jnp.float32)).astype(jnp.bfloat16)
        hidden_grad = jnp.dot(cot_seq, w_down.T, preferred_element_type=jnp.float32)
        down_part = jnp.dot(hidden.T, cot_seq, preferred_element_type=jnp.float32)
        gate_back = (hidden_grad * up_pre * sigmoid_gate * (1.0 + gate_pre * (1.0 - sigmoid_gate))).astype(jnp.bfloat16)
        up_back = (hidden_grad * silu_gate).astype(jnp.bfloat16)
        normed_mlp_grad = jnp.dot(gate_back, w_gate.T, preferred_element_type=jnp.float32) + jnp.dot(up_back, w_up.T, preferred_element_type=jnp.float32)
        gate_part = jnp.dot(normed_mlp.T, gate_back, preferred_element_type=jnp.float32)
        up_part = jnp.dot(normed_mlp.T, up_back, preferred_element_type=jnp.float32)
        mlp_back, gain_mlp_part = norm_backward(normed_mlp_grad, rms_mlp, unit_mlp, gain_mlp)
        middle_grad = cot_seq.astype(jnp.float32) + mlp_back
        middle_grad_b = middle_grad.astype(jnp.bfloat16)
        out_part = jnp.dot(attn_bf.T, middle_grad_b, preferred_element_type=jnp.float32)
        attn_back = jnp.dot(middle_grad_b, w_out.T, preferred_element_type=jnp.float32).astype(jnp.bfloat16)
        query_rot_grad, key_rot_grad, value_b_grad = attend_back(query_rot, key_rot, value_b, attn_bf, attn_back, log_total, positions)
        query_back = rotate_back(query_rot_grad, cosine, sine).reshape(SEQ_LEN, HEADS * HEAD_DIM).astype(jnp.bfloat16)
        key_back = rotate_back(key_rot_grad, cosine, sine).reshape(SEQ_LEN, KV_HEADS * HEAD_DIM).astype(jnp.bfloat16)
        value_back = value_b_grad.reshape(SEQ_LEN, KV_HEADS * HEAD_DIM).astype(jnp.bfloat16)
        normed_attn_grad = jnp.dot(query_back, w_query.T, preferred_element_type=jnp.float32)
        normed_attn_grad = normed_attn_grad + jnp.dot(key_back, w_key.T, preferred_element_type=jnp.float32)
        normed_attn_grad = normed_attn_grad + jnp.dot(value_back, w_value.T, preferred_element_type=jnp.float32)
        query_part = jnp.dot(normed_attn.T, query_back, preferred_element_type=jnp.float32)
        key_part = jnp.dot(normed_attn.T, key_back, preferred_element_type=jnp.float32)
        value_part = jnp.dot(normed_attn.T, value_back, preferred_element_type=jnp.float32)
        attn_norm_back, gain_attn_part = norm_backward(normed_attn_grad, rms_attn, unit_attn, gain_attn)
        input_back = (middle_grad + attn_norm_back).astype(jnp.bfloat16)
        parts = (gain_attn_part, gain_mlp_part, query_part, key_part, value_part, out_part, gate_part, up_part, down_part)
        new_carry = jax.tree.map(lambda summed, added: summed + added, carry, parts)
        return (new_carry, (result, input_back))
    start = (jnp.zeros((D,), jnp.float32), jnp.zeros((D,), jnp.float32), jnp.zeros(w_query.shape, jnp.float32), jnp.zeros(w_key.shape, jnp.float32), jnp.zeros(w_value.shape, jnp.float32), jnp.zeros(w_out.shape, jnp.float32), jnp.zeros(w_gate.shape, jnp.float32), jnp.zeros(w_up.shape, jnp.float32), jnp.zeros(w_down.shape, jnp.float32))
    totals, (outputs, input_grads) = lax.scan(one_sequence, start, (tokens, cotangent))
    return (outputs, input_grads, totals[0], totals[1], totals[2], totals[3], totals[4], totals[5], totals[6], totals[7], totals[8])
```

```python
import math

import jax
import jax.numpy as jnp
from jax import lax
from jax.sharding import PartitionSpec as P

HEADS = 15
KV_HEADS = 5
HEAD_DIM = 64


rope_base = 100000.0
norm_eps = 1e-05


def rope_tables(positions, half_dim):
    freq_index = jnp.arange(half_dim, dtype=jnp.float32)
    inverse = rope_base ** (-freq_index / half_dim)
    angles = positions.astype(jnp.float32)[:, None] * inverse[None, :]
    return (jnp.cos(angles), jnp.sin(angles))


def rotate(values, cosine, sine):
    half_dim = values.shape[-1] // 2
    first_half = values[..., :half_dim]
    second_half = values[..., half_dim:]
    cos_part = cosine[:, None, :]
    sin_part = sine[:, None, :]
    return jnp.concatenate(
        [
            first_half * cos_part - second_half * sin_part,
            second_half * cos_part + first_half * sin_part,
        ],
        axis=-1,
    )


def rotate_back(grads, cosine, sine):
    half_dim = grads.shape[-1] // 2
    first_half = grads[..., :half_dim]
    second_half = grads[..., half_dim:]
    cos_part = cosine[:, None, :]
    sin_part = sine[:, None, :]
    return jnp.concatenate(
        [
            first_half * cos_part + second_half * sin_part,
            second_half * cos_part - first_half * sin_part,
        ],
        axis=-1,
    )


def norm_forward(values, gain):
    inverse_rms = lax.rsqrt(jnp.mean(values * values, axis=1, keepdims=True) + norm_eps)
    scaled = values * inverse_rms
    return (inverse_rms, scaled, (scaled * gain).astype(jnp.bfloat16))


def norm_backward(grad_in, inverse_rms, scaled, gain):
    weighted = grad_in * gain
    back = inverse_rms * (weighted - scaled * jnp.mean(weighted * scaled, axis=1, keepdims=True))
    return (back, jnp.sum(grad_in * scaled, axis=0))


def dot_plain(left, right):
    return jnp.dot(left, right, preferred_element_type=jnp.float32)


def dot_right_trans(left, right):
    return lax.dot_general(
        left, right, (((1,), (1,)), ((), ())), preferred_element_type=jnp.float32
    )


def dot_left_trans(left, right):
    return lax.dot_general(
        left, right, (((0,), (0,)), ((), ())), preferred_element_type=jnp.float32
    )


def on_device(
    tokens,
    cotangent,
    block_order,
    gain_attn,
    gain_mlp,
    w_query,
    w_key,
    w_value,
    w_out,
    w_gate,
    w_up,
    w_down,
):
    rows_axes = ("seq", "fsdp")
    bf16 = jnp.bfloat16
    row_count, width = tokens.shape[1], tokens.shape[2]
    ctx_size = lax.axis_size("ctx")
    seq_len = row_count * ctx_size
    block_total = block_order.shape[0]
    block_len = seq_len // block_total
    group_size = HEADS // KV_HEADS
    kv_width = KV_HEADS * HEAD_DIM
    q_width = HEADS * HEAD_DIM
    q_cols, kv_cols, ff_cols = w_query.shape[1], w_key.shape[1], w_gate.shape[1]
    qkv_cols = q_cols + 2 * kv_cols
    attn_cols = qkv_cols + w_out.shape[1]
    scale = 1.0 / math.sqrt(HEAD_DIM)
    slot_index = jnp.arange(seq_len, dtype=jnp.int32)
    owner_hit = (slot_index // block_len)[:, None] == jnp.arange(block_total, dtype=jnp.int32)[
        None, :
    ]
    all_pos = (
        jnp.sum(jnp.where(owner_hit, block_order[None, :], 0), axis=1) * block_len
        + slot_index % block_len
    )
    own_pos = lax.dynamic_slice_in_dim(all_pos, lax.axis_index("ctx") * row_count, row_count)
    cosine, sine = rope_tables(own_pos, HEAD_DIM // 2)
    row_parts = lax.axis_size(rows_axes)

    def scatter_rows(part):
        pieces = part.reshape(row_parts, part.shape[0] // row_parts, part.shape[1])
        pieces = lax.all_to_all(pieces, rows_axes, split_axis=0, concat_axis=0, tiled=True)
        return jnp.sum(pieces.astype(jnp.float32), axis=0)

    attn_rows = lax.all_gather(
        jnp.concatenate([w_query, w_key, w_value, w_out], axis=1), rows_axes, axis=0, tiled=True
    )
    qkv_full = lax.all_gather(attn_rows[:, :qkv_cols], "ctx", axis=0)
    out_full = lax.all_gather(attn_rows[:, qkv_cols:], "ctx", axis=1, tiled=True)
    gate_up = lax.all_gather(
        jnp.concatenate([w_gate, w_up], axis=1), rows_axes, axis=0, tiled=True
    )
    gate_w, up_w = gate_up[:, :ff_cols], gate_up[:, ff_cols:]
    down_w = lax.all_to_all(
        lax.all_gather(w_down, rows_axes, axis=0, tiled=True),
        "ctx",
        split_axis=0,
        concat_axis=1,
        tiled=True,
    )
    cot_rows = cotangent[0]
    cot_all = lax.all_gather(cot_rows, "ctx", axis=0, tiled=True)

    token_f32 = tokens[0].astype(jnp.float32)
    rms_attn, unit_attn, normed_attn = norm_forward(token_f32, gain_attn)
    qkv = jnp.einsum("td,cdf->tcf", normed_attn, qkv_full, preferred_element_type=jnp.float32)
    query_raw = qkv[:, :, :q_cols].reshape(row_count, HEADS, HEAD_DIM)
    key_raw = qkv[:, :, q_cols : q_cols + kv_cols].reshape(row_count, KV_HEADS, HEAD_DIM)
    value_bf = qkv[:, :, q_cols + kv_cols :].reshape(row_count, kv_width).astype(bf16)
    query_rot = rotate(query_raw, cosine, sine).astype(bf16)
    key_rot = rotate(key_raw, cosine, sine).reshape(row_count, kv_width).astype(bf16)
    kv_all = lax.all_gather(
        jnp.concatenate([key_rot, value_bf], axis=1), "ctx", axis=0, tiled=True
    )
    key_block = min(1024, seq_len)
    num_blocks = seq_len // key_block
    kv_heads = kv_all.reshape(num_blocks, key_block, 2, KV_HEADS, HEAD_DIM)
    kv_heads = jnp.transpose(kv_heads, (2, 0, 3, 1, 4))
    key_blocks, value_blocks = kv_heads[0], kv_heads[1]
    pos_blocks = all_pos.reshape(num_blocks, key_block)

    def to_groups(rows):
        rows = rows.reshape(row_count, KV_HEADS, group_size, HEAD_DIM)
        return jnp.transpose(rows, (1, 2, 0, 3)).reshape(
            KV_HEADS, group_size * row_count, HEAD_DIM
        )

    def from_groups(rows):
        rows = rows.reshape(KV_HEADS, group_size, row_count, HEAD_DIM)
        return jnp.transpose(rows, (2, 0, 1, 3)).reshape(row_count, q_width)

    def dots(spec, left, right):
        return jnp.einsum(spec, left, right, preferred_element_type=jnp.float32)

    query_group = to_groups(query_rot)
    query_pos = jnp.tile(own_pos, group_size)

    def masked_scores(key_part, pos_part):
        allowed = pos_part[None, :] <= query_pos[:, None]
        scores = dots("gqd,gkd->gqk", query_group, key_part) * scale
        return jnp.where(allowed[None], scores, -jnp.inf)

    exp_sum = sum(
        jnp.sum(jnp.exp(masked_scores(key_blocks[i], pos_blocks[i])), axis=-1, keepdims=True)
        for i in range(num_blocks)
    )
    log_total = jnp.log(exp_sum)
    out_sum = sum(
        dots(
            "gqk,gkd->gqd",
            jnp.exp(masked_scores(key_blocks[i], pos_blocks[i]) - log_total).astype(bf16),
            value_blocks[i],
        )
        for i in range(num_blocks)
    )
    out_group = out_sum.astype(bf16)
    attn_bf = from_groups(out_group)
    middle = token_f32 + dot_plain(attn_bf, out_full)
    rms_mlp, unit_mlp, normed_mlp = norm_forward(middle, gain_mlp)

    normed_all = lax.all_gather(normed_mlp, "ctx", axis=0, tiled=True)
    gate_pre = dot_plain(normed_all, gate_w)
    up_pre = dot_plain(normed_all, up_w)
    sigmoid_gate = jax.nn.sigmoid(gate_pre)
    silu_gate = gate_pre * sigmoid_gate
    hidden = (silu_gate * up_pre).astype(bf16)
    hidden_grad = dot_right_trans(cot_all, down_w)
    gate_back = (
        hidden_grad * up_pre * sigmoid_gate * (1.0 + gate_pre * (1.0 - sigmoid_gate))
    ).astype(bf16)
    up_back = (hidden_grad * silu_gate).astype(bf16)
    normed_mlp_part = dot_right_trans(gate_back, gate_w) + dot_right_trans(up_back, up_w)
    normed_mlp_grad = lax.psum_scatter(
        normed_mlp_part.astype(bf16), "ctx", scatter_dimension=0, tiled=True
    )
    hidden, gate_back, up_back, normed_mlp_grad = lax.optimization_barrier(
        (hidden, gate_back, up_back, normed_mlp_grad)
    )
    normed_mlp_grad = normed_mlp_grad.astype(jnp.float32)

    mlp_back, gain_mlp_part = norm_backward(normed_mlp_grad, rms_mlp, unit_mlp, gain_mlp)
    middle_grad = cot_rows.astype(jnp.float32) + mlp_back
    middle_grad_b = middle_grad.astype(bf16)
    attn_back = dot_right_trans(middle_grad_b, out_full).astype(bf16)
    grad_group = to_groups(attn_back)
    row_delta = jnp.sum(
        grad_group.astype(jnp.float32) * out_group.astype(jnp.float32), axis=-1, keepdims=True
    )
    query_acc = 0.0
    key_pieces, value_pieces = [], []
    for i in range(num_blocks):
        probs_full = jnp.exp(masked_scores(key_blocks[i], pos_blocks[i]) - log_total)
        prob_grad = dots("gqd,gkd->gqk", grad_group, value_blocks[i])
        score_grad = (probs_full * (prob_grad - row_delta) * scale).astype(bf16)
        query_acc = query_acc + dots("gqk,gkd->gqd", score_grad, key_blocks[i])
        key_pieces.append(dots("gqk,gqd->gkd", score_grad, query_group).astype(bf16))
        value_pieces.append(dots("gqk,gqd->gkd", probs_full.astype(bf16), grad_group).astype(bf16))
    kv_pieces = jnp.stack([jnp.stack(key_pieces), jnp.stack(value_pieces)])
    kv_pieces = jnp.transpose(kv_pieces, (1, 3, 0, 2, 4)).reshape(seq_len, 2 * kv_width)
    kv_own = lax.psum_scatter(kv_pieces, "ctx", scatter_dimension=0, tiled=True)

    output_part = dot_plain(hidden, down_w).astype(bf16)
    output_own = lax.psum_scatter(output_part, "ctx", scatter_dimension=0, tiled=True)
    result = (middle + output_own.astype(jnp.float32)).astype(bf16)
    gate_up_part = jnp.concatenate(
        [dot_left_trans(normed_all, gate_back), dot_left_trans(normed_all, up_back)], axis=1
    ).astype(bf16)
    fin_gate_up = scatter_rows(gate_up_part)
    down_part = lax.all_to_all(
        dot_left_trans(hidden, cot_all).astype(bf16),
        "ctx",
        split_axis=1,
        concat_axis=0,
        tiled=True,
    )
    fin_down = scatter_rows(down_part)
    out_mid = lax.psum_scatter(
        dot_left_trans(attn_bf, middle_grad_b).astype(bf16),
        "ctx",
        scatter_dimension=1,
        tiled=True,
    )

    query_back = rotate_back(
        from_groups(query_acc).reshape(row_count, HEADS, HEAD_DIM), cosine, sine
    ).astype(bf16)
    key_back = rotate_back(
        kv_own[:, :kv_width].astype(jnp.float32).reshape(row_count, KV_HEADS, HEAD_DIM),
        cosine,
        sine,
    ).astype(bf16)
    qkv_back = jnp.concatenate(
        [
            query_back.reshape(row_count, ctx_size, q_cols),
            key_back.reshape(row_count, ctx_size, kv_cols),
            kv_own[:, kv_width:].reshape(row_count, ctx_size, kv_cols),
        ],
        axis=2,
    )
    normed_attn_grad = dots("tcf,cdf->td", qkv_back, qkv_full)
    qkv_part = dots("td,tcf->cdf", normed_attn, qkv_back).astype(bf16)
    qkv_mid = lax.psum_scatter(qkv_part, "ctx", scatter_dimension=0, tiled=False)
    fin_attn = scatter_rows(jnp.concatenate([qkv_mid, out_mid], axis=1))
    attn_norm_back, gain_attn_part = norm_backward(normed_attn_grad, rms_attn, unit_attn, gain_attn)
    input_back = (middle_grad + attn_norm_back).astype(bf16)
    gain_attn_sum, gain_mlp_sum = lax.psum((gain_attn_part, gain_mlp_part), ("seq", "fsdp", "ctx"))
    return (
        result.reshape(1, row_count, width),
        input_back.reshape(1, row_count, width),
        gain_attn_sum,
        gain_mlp_sum,
        fin_attn[:, :q_cols],
        fin_attn[:, q_cols : q_cols + kv_cols],
        fin_attn[:, q_cols + kv_cols : qkv_cols],
        fin_attn[:, qkv_cols:attn_cols],
        fin_gate_up[:, :ff_cols],
        fin_gate_up[:, ff_cols:],
        fin_down,
    )


def solution(mesh):
    return jax.shard_map(
        on_device,
        mesh=mesh,
        in_specs=(
            P(("seq", "fsdp"), "ctx", None),
            P(("seq", "fsdp"), "ctx", None),
            P(),
            P(),
            P(),
            P(("seq", "fsdp"), "ctx"),
            P(("seq", "fsdp"), "ctx"),
            P(("seq", "fsdp"), "ctx"),
            P(("seq", "fsdp"), "ctx"),
            P(("seq", "fsdp"), "ctx"),
            P(("seq", "fsdp"), "ctx"),
            P(("seq", "fsdp"), "ctx"),
        ),
        out_specs=(
            P(("seq", "fsdp"), "ctx", None),
            P(("seq", "fsdp"), "ctx", None),
            P(),
            P(),
            P(("seq", "fsdp"), "ctx"),
            P(("seq", "fsdp"), "ctx"),
            P(("seq", "fsdp"), "ctx"),
            P(("seq", "fsdp"), "ctx"),
            P(("seq", "fsdp"), "ctx"),
            P(("seq", "fsdp"), "ctx"),
            P(("seq", "fsdp"), "ctx"),
        ),
        check_vma=False,
    )
```

```python
import math

import jax
import jax.numpy as jnp
from jax import lax
from jax.sharding import PartitionSpec as P

HEADS = 15
KV_HEADS = 5
HEAD_DIM = 64


rope_base = 100000.0
norm_eps = 1e-05


def rope_tables(positions, half_dim):
    freq_index = jnp.arange(half_dim, dtype=jnp.float32)
    inverse = rope_base ** (-freq_index / half_dim)
    angles = positions.astype(jnp.float32)[:, None] * inverse[None, :]
    return (jnp.cos(angles), jnp.sin(angles))


def rotate(values, cosine, sine):
    half_dim = values.shape[-1] // 2
    first_half = values[..., :half_dim]
    second_half = values[..., half_dim:]
    cos_part = cosine[:, None, :]
    sin_part = sine[:, None, :]
    return jnp.concatenate(
        [
            first_half * cos_part - second_half * sin_part,
            second_half * cos_part + first_half * sin_part,
        ],
        axis=-1,
    )


def rotate_back(grads, cosine, sine):
    half_dim = grads.shape[-1] // 2
    first_half = grads[..., :half_dim]
    second_half = grads[..., half_dim:]
    cos_part = cosine[:, None, :]
    sin_part = sine[:, None, :]
    return jnp.concatenate(
        [
            first_half * cos_part + second_half * sin_part,
            second_half * cos_part - first_half * sin_part,
        ],
        axis=-1,
    )


def norm_forward(values, gain):
    inverse_rms = lax.rsqrt(jnp.mean(values * values, axis=1, keepdims=True) + norm_eps)
    scaled = values * inverse_rms
    return (inverse_rms, scaled, (scaled * gain).astype(jnp.bfloat16))


def norm_backward(grad_in, inverse_rms, scaled, gain):
    weighted = grad_in * gain
    back = inverse_rms * (weighted - scaled * jnp.mean(weighted * scaled, axis=1, keepdims=True))
    return (back, jnp.sum(grad_in * scaled, axis=0))


def dot_plain(left, right):
    return jnp.dot(left, right, preferred_element_type=jnp.float32)


def dot_right_trans(left, right):
    return lax.dot_general(
        left, right, (((1,), (1,)), ((), ())), preferred_element_type=jnp.float32
    )


def dot_left_trans(left, right):
    return lax.dot_general(
        left, right, (((0,), (0,)), ((), ())), preferred_element_type=jnp.float32
    )


def on_device(
    tokens,
    cotangent,
    block_order,
    gain_attn,
    gain_mlp,
    w_query,
    w_key,
    w_value,
    w_out,
    w_gate,
    w_up,
    w_down,
):
    rows_axes = ("seq", "fsdp")
    bf16 = jnp.bfloat16
    row_count, width = tokens.shape[1], tokens.shape[2]
    ctx_size = lax.axis_size("ctx")
    seq_len = row_count * ctx_size
    block_total = block_order.shape[0]
    block_len = seq_len // block_total
    group_size = HEADS // KV_HEADS
    kv_width = KV_HEADS * HEAD_DIM
    q_width = HEADS * HEAD_DIM
    q_cols, kv_cols, ff_cols = w_query.shape[1], w_key.shape[1], w_gate.shape[1]
    qkv_cols = q_cols + 2 * kv_cols
    attn_cols = qkv_cols + w_out.shape[1]
    scale = 1.0 / math.sqrt(HEAD_DIM)
    slot_index = jnp.arange(seq_len, dtype=jnp.int32)
    owner_hit = (slot_index // block_len)[:, None] == jnp.arange(block_total, dtype=jnp.int32)[
        None, :
    ]
    all_pos = (
        jnp.sum(jnp.where(owner_hit, block_order[None, :], 0), axis=1) * block_len
        + slot_index % block_len
    )
    own_pos = lax.dynamic_slice_in_dim(all_pos, lax.axis_index("ctx") * row_count, row_count)
    cosine, sine = rope_tables(own_pos, HEAD_DIM // 2)
    row_parts = lax.axis_size(rows_axes)

    def scatter_rows(part):
        pieces = part.reshape(row_parts, part.shape[0] // row_parts, part.shape[1])
        pieces = lax.all_to_all(pieces, rows_axes, split_axis=0, concat_axis=0, tiled=True)
        return jnp.sum(pieces.astype(jnp.float32), axis=0)

    attn_rows = lax.all_gather(
        jnp.concatenate([w_query, w_key, w_value, w_out], axis=1), rows_axes, axis=0, tiled=True
    )
    cot_rows = cotangent[0]
    cot_all = lax.all_gather(cot_rows, "ctx", axis=0, tiled=True)
    attn_rows, cot_all = lax.optimization_barrier((attn_rows, cot_all))
    attn_full = lax.all_gather(attn_rows, "ctx", axis=0)
    qkv_full = attn_full[:, :, :qkv_cols]
    out_full = jnp.transpose(attn_full[:, :, qkv_cols:], (1, 0, 2)).reshape(q_width, width)
    down_rows = lax.all_gather(w_down, rows_axes, axis=0, tiled=True)
    down_w = lax.all_to_all(down_rows, "ctx", split_axis=0, concat_axis=1, tiled=True)
    gate_in, _ = lax.optimization_barrier((w_gate, down_w))
    gate_w = lax.all_gather(gate_in, rows_axes, axis=0, tiled=True)
    up_in, _ = lax.optimization_barrier((w_up, gate_w))
    up_w = lax.all_gather(up_in, rows_axes, axis=0, tiled=True)
    token_f32 = tokens[0].astype(jnp.float32)
    rms_attn, unit_attn, normed_attn = norm_forward(token_f32, gain_attn)
    normed_attn, gate_w, up_w, down_w = lax.optimization_barrier(
        (normed_attn, gate_w, up_w, down_w)
    )
    qkv = jnp.einsum("td,cdf->tcf", normed_attn, qkv_full, preferred_element_type=jnp.float32)
    query_raw = qkv[:, :, :q_cols].reshape(row_count, HEADS, HEAD_DIM)
    key_raw = qkv[:, :, q_cols : q_cols + kv_cols].reshape(row_count, KV_HEADS, HEAD_DIM)
    value_bf = qkv[:, :, q_cols + kv_cols :].reshape(row_count, kv_width).astype(bf16)
    query_rot = rotate(query_raw, cosine, sine).astype(bf16)
    key_rot = rotate(key_raw, cosine, sine).reshape(row_count, kv_width).astype(bf16)
    kv_all = lax.all_gather(
        jnp.concatenate([key_rot, value_bf], axis=1), "ctx", axis=0, tiled=True
    )
    key_block = min(1024, seq_len)
    num_blocks = seq_len // key_block
    kv_heads = kv_all.reshape(num_blocks, key_block, 2, KV_HEADS, HEAD_DIM)
    kv_heads = jnp.transpose(kv_heads, (2, 0, 3, 1, 4))
    key_blocks, value_blocks = kv_heads[0], kv_heads[1]
    pos_blocks = all_pos.reshape(num_blocks, key_block)

    def to_groups(rows):
        rows = rows.reshape(row_count, KV_HEADS, group_size, HEAD_DIM)
        return jnp.transpose(rows, (1, 2, 0, 3)).reshape(
            KV_HEADS, group_size * row_count, HEAD_DIM
        )

    def from_groups(rows):
        rows = rows.reshape(KV_HEADS, group_size, row_count, HEAD_DIM)
        return jnp.transpose(rows, (2, 0, 1, 3)).reshape(row_count, q_width)

    def dots(spec, left, right):
        return jnp.einsum(spec, left, right, preferred_element_type=jnp.float32)

    query_group = to_groups(query_rot)
    query_pos = jnp.tile(own_pos, group_size)

    def masked_scores(key_part, pos_part):
        allowed = pos_part[None, :] <= query_pos[:, None]
        scores = dots("gqd,gkd->gqk", query_group, key_part) * scale
        return jnp.where(allowed[None], scores, -jnp.inf)

    exp_sum = sum(
        jnp.sum(jnp.exp(masked_scores(key_blocks[i], pos_blocks[i])), axis=-1, keepdims=True)
        for i in range(num_blocks)
    )
    log_total = jnp.log(exp_sum)
    out_sum = sum(
        dots(
            "gqk,gkd->gqd",
            jnp.exp(masked_scores(key_blocks[i], pos_blocks[i]) - log_total).astype(bf16),
            value_blocks[i],
        )
        for i in range(num_blocks)
    )
    out_group = out_sum.astype(bf16)
    attn_bf = from_groups(out_group)
    middle = token_f32 + dot_plain(attn_bf, out_full)
    rms_mlp, unit_mlp, normed_mlp = norm_forward(middle, gain_mlp)

    normed_all = lax.all_gather(normed_mlp, "ctx", axis=0, tiled=True)
    gate_pre = dot_plain(normed_all, gate_w)
    up_pre = dot_plain(normed_all, up_w)
    sigmoid_gate = jax.nn.sigmoid(gate_pre)
    silu_gate = gate_pre * sigmoid_gate
    hidden = (silu_gate * up_pre).astype(bf16)
    hidden_grad = dot_right_trans(cot_all, down_w)
    gate_back = (
        hidden_grad * up_pre * sigmoid_gate * (1.0 + gate_pre * (1.0 - sigmoid_gate))
    ).astype(bf16)
    up_back = (hidden_grad * silu_gate).astype(bf16)
    normed_mlp_part = dot_right_trans(gate_back, gate_w) + dot_right_trans(up_back, up_w)
    normed_mlp_grad = lax.psum_scatter(
        normed_mlp_part.astype(bf16), "ctx", scatter_dimension=0, tiled=True
    )
    hidden, gate_back, up_back, normed_mlp_grad = lax.optimization_barrier(
        (hidden, gate_back, up_back, normed_mlp_grad)
    )
    normed_mlp_grad = normed_mlp_grad.astype(jnp.float32)

    mlp_back, gain_mlp_part = norm_backward(normed_mlp_grad, rms_mlp, unit_mlp, gain_mlp)
    middle_grad = cot_rows.astype(jnp.float32) + mlp_back
    middle_grad_b = middle_grad.astype(bf16)
    attn_back = dot_right_trans(middle_grad_b, out_full).astype(bf16)
    grad_group = to_groups(attn_back)
    row_delta = jnp.sum(
        grad_group.astype(jnp.float32) * out_group.astype(jnp.float32), axis=-1, keepdims=True
    )
    query_acc = 0.0
    key_pieces, value_pieces = [], []
    for i in range(num_blocks):
        probs_full = jnp.exp(masked_scores(key_blocks[i], pos_blocks[i]) - log_total)
        prob_grad = dots("gqd,gkd->gqk", grad_group, value_blocks[i])
        score_grad = (probs_full * (prob_grad - row_delta) * scale).astype(bf16)
        query_acc = query_acc + dots("gqk,gkd->gqd", score_grad, key_blocks[i])
        key_pieces.append(dots("gqk,gqd->gkd", score_grad, query_group).astype(bf16))
        value_pieces.append(dots("gqk,gqd->gkd", probs_full.astype(bf16), grad_group).astype(bf16))
    kv_pieces = jnp.stack([jnp.stack(key_pieces), jnp.stack(value_pieces)])
    kv_pieces = jnp.transpose(kv_pieces, (1, 3, 0, 2, 4)).reshape(seq_len, 2 * kv_width)
    kv_pieces, hidden, gate_back, up_back, middle_late = lax.optimization_barrier(
        (kv_pieces, hidden, gate_back, up_back, middle_grad_b)
    )
    kv_own = lax.psum_scatter(kv_pieces, "ctx", scatter_dimension=0, tiled=True)

    gate_up_part = jnp.concatenate(
        [dot_left_trans(normed_all, gate_back), dot_left_trans(normed_all, up_back)], axis=1
    ).astype(bf16)
    fin_gate_up = scatter_rows(gate_up_part)
    down_part = lax.all_to_all(
        dot_left_trans(hidden, cot_all).astype(bf16),
        "ctx",
        split_axis=1,
        concat_axis=0,
        tiled=True,
    )
    fin_down = scatter_rows(down_part)
    out_part = dots(
        "td,tcf->cdf", attn_bf, middle_late.reshape(row_count, ctx_size, width // ctx_size)
    ).astype(bf16)
    out_pieces = lax.all_to_all(out_part, "ctx", split_axis=0, concat_axis=0, tiled=True)
    out_mid = jnp.sum(out_pieces.astype(jnp.float32), axis=0).astype(bf16)

    query_back = rotate_back(
        from_groups(query_acc).reshape(row_count, HEADS, HEAD_DIM), cosine, sine
    ).astype(bf16)
    key_back = rotate_back(
        kv_own[:, :kv_width].astype(jnp.float32).reshape(row_count, KV_HEADS, HEAD_DIM),
        cosine,
        sine,
    ).astype(bf16)
    qkv_back = jnp.concatenate(
        [
            query_back.reshape(row_count, ctx_size, q_cols),
            key_back.reshape(row_count, ctx_size, kv_cols),
            kv_own[:, kv_width:].reshape(row_count, ctx_size, kv_cols),
        ],
        axis=2,
    )
    normed_attn_grad = dots("tcf,cdf->td", qkv_back, qkv_full)
    qkv_part = dots("td,tcf->cdf", normed_attn, qkv_back).astype(bf16)
    qkv_mid = lax.psum_scatter(qkv_part, "ctx", scatter_dimension=0, tiled=False)
    output_part, qkv_mid = lax.optimization_barrier(
        (dot_plain(hidden, down_w).astype(bf16), qkv_mid)
    )
    output_own = lax.psum_scatter(output_part, "ctx", scatter_dimension=0, tiled=True)
    result = (middle + output_own.astype(jnp.float32)).astype(bf16)
    fin_attn = scatter_rows(jnp.concatenate([qkv_mid, out_mid], axis=1))
    attn_norm_back, gain_attn_part = norm_backward(normed_attn_grad, rms_attn, unit_attn, gain_attn)
    input_back = (middle_grad + attn_norm_back).astype(bf16)
    gain_parts = lax.all_gather(
        jnp.stack([gain_attn_part, gain_mlp_part]), ("seq", "fsdp", "ctx"), axis=0
    )
    gain_attn_sum, gain_mlp_sum = jnp.sum(gain_parts, axis=0)
    return (
        result.reshape(1, row_count, width),
        input_back.reshape(1, row_count, width),
        gain_attn_sum,
        gain_mlp_sum,
        fin_attn[:, :q_cols],
        fin_attn[:, q_cols : q_cols + kv_cols],
        fin_attn[:, q_cols + kv_cols : qkv_cols],
        fin_attn[:, qkv_cols:attn_cols],
        fin_gate_up[:, :ff_cols],
        fin_gate_up[:, ff_cols:],
        fin_down,
    )


def solution(mesh):
    return jax.shard_map(
        on_device,
        mesh=mesh,
        in_specs=(
            P(("seq", "fsdp"), "ctx", None),
            P(("seq", "fsdp"), "ctx", None),
            P(),
            P(),
            P(),
            P(("seq", "fsdp"), "ctx"),
            P(("seq", "fsdp"), "ctx"),
            P(("seq", "fsdp"), "ctx"),
            P(("seq", "fsdp"), "ctx"),
            P(("seq", "fsdp"), "ctx"),
            P(("seq", "fsdp"), "ctx"),
            P(("seq", "fsdp"), "ctx"),
        ),
        out_specs=(
            P(("seq", "fsdp"), "ctx", None),
            P(("seq", "fsdp"), "ctx", None),
            P(),
            P(),
            P(("seq", "fsdp"), "ctx"),
            P(("seq", "fsdp"), "ctx"),
            P(("seq", "fsdp"), "ctx"),
            P(("seq", "fsdp"), "ctx"),
            P(("seq", "fsdp"), "ctx"),
            P(("seq", "fsdp"), "ctx"),
            P(("seq", "fsdp"), "ctx"),
        ),
        check_vma=False,
    )
```
